256 devices in a mesh: gx: 16 (over y, x_hi, core), gy: 16 (over z, x_lo).
Axes of the slice: x: 4 (x_hi: 2, x_lo: 2; x = x_hi * 2 + x_lo), y: 4, z: 8, core: 2. Of those that a mesh axis runs over, the one named last changes fastest.
Arguments:
- right_side: float32 [6, 64, 65536], P(None, 'gx', 'gy'), may hold values from -16 to 16
- flux_jac: float32 [3, 6, 6, 64, 1024], P(None, None, None, 'gx', 'gy'), may hold values from -0.3 to 0.3
- wave_speed: float32 [64, 1024], P('gx', 'gy'), may hold values from 0.3 to 1.5
- source: float32 [6, 64, 65536], P(None, 'gx', 'gy'), may hold values from 6 to 12
- wall_flag: int32 [64, 256], P('gx', 'gy'), may hold values 0 or 1
- turbine_elem: int32 [512], replicated, may hold values from 0 to 65535
- disc_coef: float32 [512], replicated, may hold values from 2 to 8
Outputs:
- adjoint_solution: float32 [6, 64, 65536], P(None, 'gx', 'gy')
The draws below stay inside these ranges and needn't reach their ends.
All inputs are finite; a program needn't handle non-finite values. No bound on the sum of `wall_flag` on one device may be relied on, other than what follows from the above.
Results may differ from the reference program's by a relative error of at most 0.0003.
Values sent between devices are 32-bit elements; how exact they have to be, the bound alone decides.
No kernel may reach another device: no remote copies, remote signals or barrier semaphores. Data moves between devices by JAX's collectives and lax.ppermute only.
A program may use at most 64 MiB of HBM per device.

```python
import math
import jax
import jax.numpy as jnp
import numpy as np
from jax import lax

EZ = 4
ITERS = 3
NX = 64
NY = 256
NTURB = 512


def draw_right_side(key, part):
    first_key = jax.random.fold_in(key, 0)
    shape_full = (6, NX, NY * EZ * 64)
    row_pos = lax.broadcasted_iota(jnp.float32, (1, NX, 1), 1)
    stream_ramp = 1.0 + 2.0 * row_pos / max(NX - 1, 1)
    basic_draw = jnp.clip(jax.random.normal(first_key, shape_full, jnp.float32), -4.0, 4.0)
    return basic_draw * stream_ramp


def touch_ends(values, rng, least, top_value):
    extent = values.shape
    spot = [jax.random.randint(jax.random.fold_in(rng, axis), (), 0, extent[axis]) for axis in range(len(extent))]
    values = values.at[tuple(spot)].set(least)
    longest = extent.index(max(extent))
    spot[longest] = (spot[longest] + 1) % extent[longest]
    return values.at[tuple(spot)].set(top_value)


def level_of(key, shape, pieces, smallest, largest):
    level, own = 1.0, jax.random.fold_in(key, 6)
    for dim, shards_of in pieces:
        steps = jnp.exp(jax.random.uniform(jax.random.fold_in(own, dim), (shards_of,), jnp.float32, smallest / len(pieces), largest / len(pieces)))
        level = level * jnp.repeat(steps, shape[dim] // shards_of).reshape([-1 if axis == dim else 1 for axis in range(len(shape))])
    return level


def gaussian(own_key, dims, scale, reach, pieces=(), kind=jnp.bfloat16):
    entries = scale * jax.random.normal(own_key, dims, jnp.float32)
    if pieces:
        entries = entries * level_of(own_key, dims, pieces, -0.22, 0.18)
    return jnp.clip(entries, -reach, reach).astype(kind)


def setup_inputs(seed: int = 0) -> dict:
    seeds = jax.random.split(jax.random.key(seed), 8)
    return {
        "right_side": draw_right_side(jax.random.fold_in(seeds[7], 71), 0),
        "flux_jac": gaussian(seeds[1], (3, 6, 6, NX, NY * EZ), 0.05, 0.3, ((3, 16), (4, 16)), jnp.float32),
        "wave_speed": jnp.clip(jnp.exp(math.log(1.5) - 1.60943787 * jax.random.uniform(seeds[2], (NX, NY * EZ), jnp.float32) ** level_of(seeds[2], (NX, NY * EZ), ((0, 16), (1, 16)), -0.2, 0.2)), 0.3, 1.5),
        "source": jnp.clip(6.0 + 6.0 * jax.random.uniform(seeds[3], (6, NX, NY * EZ * 64), jnp.float32) ** level_of(seeds[3], (6, NX, NY * EZ * 64), ((1, 16), (2, 16)), -0.2, 0.2), 6.0, 12.0),
        "wall_flag": touch_ends((jax.random.randint(seeds[4], (NX, NY), 0, 2) < 1).astype(jnp.int32), jax.random.fold_in(seeds[4], 1), 0, 1),
        "turbine_elem": touch_ends(jax.random.randint(seeds[5], (NTURB,), 0, NX * NY * EZ), jax.random.fold_in(seeds[5], 1), 0, (NX * NY * EZ) - 1).astype(jnp.int32),
        "disc_coef": jnp.clip(jnp.exp(jax.random.uniform(seeds[6], (NTURB,), jnp.float32, math.log(2.0), math.log(8.0))), 2.0, 8.0),
    }


LIFT_HALF = 3.0
EXACT = lax.Precision.HIGHEST

def gll_derivative():
    points = np.array([-1.0, -1.0 / math.sqrt(5.0), 1.0 / math.sqrt(5.0), 1.0])
    bary_weights = np.array([1.0 / np.prod([points[j] - points[k] for k in range(4) if k != j]) for j in range(4)])
    derivative = np.zeros((4, 4))
    for i in range(4):
        for j in range(4):
            if i != j:
                derivative[i, j] = bary_weights[j] / bary_weights[i] / (points[i] - points[j])
        derivative[i, i] = -np.sum(derivative[i])
    return derivative

def node_triple(node_idx):
    return (node_idx % 4, node_idx // 4 % 4, node_idx // 16)

def volume_tables(layers):
    derivative = gll_derivative()
    tables = np.zeros((3, 64 * layers, 64 * layers), np.float32)
    for direction in range(3):
        for layer_idx in range(layers):
            for row_idx in range(64):
                row_parts = node_triple(row_idx)
                for col_idx in range(64):
                    col_parts = node_triple(col_idx)
                    matching = all((row_parts[k] == col_parts[k] for k in range(3) if k != direction))
                    if matching:
                        tables[direction, layer_idx * 64 + row_idx, layer_idx * 64 + col_idx] = derivative[row_parts[direction], col_parts[direction]]
    return tables

def face_tables(layers):
    tables = np.zeros((3, 64 * layers, 32 * layers), np.float32)
    for direction in range(3):
        for layer_idx in range(layers):
            for node_idx in range(64):
                node_parts = node_triple(node_idx)
                others = [node_parts[k] for k in range(3) if k != direction]
                position = others[1] * 4 + others[0]
                for side_idx in range(2):
                    if node_parts[direction] == 3 * side_idx:
                        tables[direction, layer_idx * 64 + node_idx, side_idx * 16 * layers + layer_idx * 16 + position] = 1.0
    return tables

def layer_shift(layers):
    width = 16 * layers
    table = np.zeros((2 * width, 2 * width), np.float32)
    for layer_idx in range(layers):
        for position in range(16):
            if layer_idx >= 1:
                table[width + (layer_idx - 1) * 16 + position, layer_idx * 16 + position] = 1.0
            if layer_idx + 1 < layers:
                table[(layer_idx + 1) * 16 + position, width + layer_idx * 16 + position] = 1.0
    return table

def local_traces(field4, table):
    return jnp.matmul(field4, table, precision=EXACT)

def neighbour_traces(traces, lower, upper, axis_dim):
    half_width = traces.shape[-1] // 2
    length = traces.shape[axis_dim]
    below_trace = jnp.concatenate([lower, lax.slice_in_dim(traces[..., half_width:], 0, length - 1, axis=axis_dim)], axis_dim)
    above_trace = jnp.concatenate([lax.slice_in_dim(traces[..., :half_width], 1, length, axis=axis_dim), upper], axis_dim)
    return jnp.concatenate([below_trace, above_trace], -1)

def face_term(traces, neighbours, matrix, wave_speed, layers):
    row_count, col_count = (traces.shape[1], traces.shape[2])
    width = 16 * layers
    joined = (traces + neighbours).reshape(6, row_count, col_count, 2, layers, 16)
    grid_mat = matrix.reshape(6, 6, row_count, col_count, layers)
    mixed_vals = jnp.einsum('ijxyl,ixysln->jxysln', grid_mat, joined, precision=EXACT).reshape(traces.shape)
    orient_sign = jnp.concatenate([jnp.ones((width,), traces.dtype), -jnp.ones((width,), traces.dtype)])
    speeds = jnp.broadcast_to(wave_speed.reshape(row_count, col_count, 1, layers, 1), (row_count, col_count, 2, layers, 16)).reshape(row_count, col_count, 2 * width)
    return LIFT_HALF * (orient_sign * mixed_vals + speeds * (traces - neighbours))

def volume_term(field4, table, matrix, layers):
    row_count, col_count = (field4.shape[1], field4.shape[2])
    slopes = jnp.matmul(field4, table, precision=EXACT).reshape(6, row_count, col_count, layers, 64)
    grid_mat = matrix.reshape(6, 6, row_count, col_count, layers)
    return jnp.einsum('ijxyl,ixyln->jxyln', grid_mat, slopes, precision=EXACT).reshape(field4.shape)

def assemble(field4, traces3, neighbours3, flux_jac, wave_speed, diagonal4, wall_factor, vol_tabs, face_tabs, layers):
    result = diagonal4 * field4
    for direction in range(3):
        result = result + volume_term(field4, vol_tabs[direction], flux_jac[direction], layers)
        contrib = face_term(traces3[direction], neighbours3[direction], flux_jac[direction], wave_speed, layers)
        if direction == 2:
            contrib = contrib * wall_factor
        result = result + jnp.matmul(contrib, face_tabs[direction].T, precision=EXACT)
    return result

def build_diagonal(source4, kappa, layers):
    row_count, col_count = (source4.shape[1], source4.shape[2])
    per_node = jnp.broadcast_to(kappa.reshape(row_count, col_count, layers, 1), (row_count, col_count, layers, 64)).reshape(row_count, col_count, 64 * layers)
    momentum = jnp.array([0.0, 1.0, 1.0, 1.0, 0.0, 0.0], source4.dtype).reshape(6, 1, 1, 1)
    return source4 + momentum * per_node

def build_wall(wall_flag, layers, dtype):
    column = jnp.arange(32 * layers)
    lowest = (column < 16).astype(dtype)
    return 1.0 + wall_flag.astype(dtype)[:, :, None] * lowest

def least_squares(hessenberg, beta_norm, iters):
    cosines, sines, triangle = ([], [], [])
    target = [beta_norm] + [0.0 * beta_norm for index in range(iters)]
    for j in range(iters):
        column = list(hessenberg[j])
        for i in range(j):
            first_val, second_val = (column[i], column[i + 1])
            column[i] = cosines[i] * first_val + sines[i] * second_val
            column[i + 1] = -sines[i] * first_val + cosines[i] * second_val
        radius = jnp.sqrt(column[j] * column[j] + column[j + 1] * column[j + 1])
        cosines.append(column[j] / radius)
        sines.append(column[j + 1] / radius)
        column[j] = radius
        triangle.append(column[:j + 1])
        previous = target[j]
        target[j] = cosines[j] * previous
        target[j + 1] = -sines[j] * previous
    combination = [None] * iters
    for j in reversed(range(iters)):
        partial_sum = target[j]
        for k in range(j + 1, iters):
            partial_sum = partial_sum - triangle[k][j] * combination[k]
        combination[j] = partial_sum / triangle[j][j]
    return combination

def reference(right_side, flux_jac, wave_speed, source, wall_flag, turbine_elem, disc_coef):
    layers = EZ
    vol_tabs = jnp.asarray(volume_tables(layers))
    face_tabs = jnp.asarray(face_tables(layers))
    z_table = jnp.asarray(layer_shift(layers))
    half_width = 16 * layers
    kappa = jnp.zeros((NX * NY * EZ,), right_side.dtype).at[turbine_elem].add(disc_coef).reshape(NX, NY * EZ)
    diagonal4 = build_diagonal(source.reshape(6, NX, NY, 64 * layers), kappa, layers)
    wall_factor = build_wall(wall_flag, layers, right_side.dtype)

    def operate(field):
        field4 = field.reshape(6, NX, NY, 64 * layers)
        trace_x = local_traces(field4, face_tabs[0])
        trace_y = local_traces(field4, face_tabs[1])
        trace_z = local_traces(field4, face_tabs[2])
        empty = jnp.zeros((6, 1, NY, half_width), field.dtype)
        near_x = neighbour_traces(trace_x, empty, empty, 1)
        near_y = neighbour_traces(trace_y, trace_y[:, :, -1:, half_width:], trace_y[:, :, :1, :half_width], 2)
        near_z = jnp.matmul(trace_z, z_table, precision=EXACT)
        result = assemble(field4, (trace_x, trace_y, trace_z), (near_x, near_y, near_z), flux_jac, wave_speed, diagonal4, wall_factor, vol_tabs, face_tabs, layers)
        return result.reshape(field.shape)
    beta_norm = jnp.sqrt(jnp.sum(right_side * right_side) + 1e-06)
    krylov = [right_side / beta_norm]
    hessenberg = []
    for step in range(ITERS):
        image = operate(krylov[step])
        column = [jnp.sum(image * vector) for vector in krylov]
        remainder = image
        for vector, height in zip(krylov, column):
            remainder = remainder - height * vector
        below_norm = jnp.sqrt(jnp.sum(remainder * remainder) + 1e-06)
        column.append(below_norm)
        hessenberg.append(column)
        if step + 1 < ITERS:
            krylov.append(remainder / below_norm)
    combination = least_squares(hessenberg, beta_norm, ITERS)
    solution = combination[0] * krylov[0]
    for j in range(1, ITERS):
        solution = solution + combination[j] * krylov[j]
    return solution
```

```python
import math

import jax
import jax.numpy as jnp
import numpy as np
from jax import lax
from jax.experimental import pallas as pl
from jax.experimental.pallas import tpu as pltpu
from jax.sharding import PartitionSpec as P

EPS = 1e-06
SHIFT = 12.0
SLOTS = (0, 1, 3, 2)
EXACT = lax.Precision.HIGHEST
PARAMS = pltpu.CompilerParams(vmem_limit_bytes=24 * 2**20)
FIELD = jax.ShapeDtypeStruct((6, 16, 8, 128), jnp.float32)
XPACK = jax.ShapeDtypeStruct((6, 8, 128), jnp.float32)
YPACK = jax.ShapeDtypeStruct((2, 8, 128), jnp.float32)
DOTS = jax.ShapeDtypeStruct((8, 128), jnp.float32)


def gll_derivative():
    points = np.array([-1.0, -1.0 / math.sqrt(5.0), 1.0 / math.sqrt(5.0), 1.0])
    bary_weights = np.array(
        [1.0 / np.prod([points[j] - points[k] for k in range(4) if k != j]) for j in range(4)]
    )
    derivative = np.zeros((4, 4))
    for i in range(4):
        for j in range(4):
            if i != j:
                derivative[i, j] = bary_weights[j] / bary_weights[i] / (points[i] - points[j])
        derivative[i, i] = -np.sum(derivative[i])
    return derivative


DHAT = gll_derivative()


def lanes():
    return lax.broadcasted_iota(jnp.int32, (8, 128), 1)


def sublanes():
    return lax.broadcasted_iota(jnp.int32, (8, 128), 0)


def roll(value, by, axis):
    by = by % value.shape[axis]
    return pltpu.roll(value, by, axis) if by else value


def block_of(khalf, c):
    return (SLOTS.index(c) * 2 + khalf) * 16


def pack_faces(get, parity_x, parity_y, xa_ref, xb_ref, ya_ref, yb_ref):
    lane = lanes()
    for v in range(6):
        plus = minus = jnp.zeros((8, 128), jnp.float32)
        for b in range(4):
            here = lane % 4 == b
            plus = jnp.where(here, roll(get(v, b * 4 + 3), b - 3, 1), plus)
            minus = jnp.where(here, roll(get(v, b * 4), b, 1), minus)
        xa_ref[v] = jnp.where(parity_x == 0, plus, minus)
        xb_ref[v] = jnp.where(parity_x == 0, minus, plus)
    for half in range(2):
        plus = minus = jnp.zeros((8, 128), jnp.float32)
        for v in range(half * 4, min(half * 4 + 4, 6)):
            for a in range(4):
                slot = (v % 4) * 4 + a
                here = lane // 8 == slot
                plus = jnp.where(here, roll(get(v, 12 + a), 8 + 8 * slot, 1), plus)
                minus = jnp.where(here, roll(get(v, a), 8 * slot, 1), minus)
        ya_ref[half] = jnp.where(parity_y == 0, plus, minus)
        yb_ref[half] = jnp.where(parity_y == 0, minus, plus)


def into_layout(matrix, stage_ref):
    turned = matrix.T
    for khalf in range(2):
        for c in range(4):
            source = khalf * 64 + c * 16
            target = block_of(khalf, c)
            stage_ref[target : target + 16, :] = turned[source : source + 16, :]


def start_kernel(rhs_ref, w_ref, xa_ref, xb_ref, ya_ref, yb_ref, stage_ref):
    for v in range(6):
        into_layout(rhs_ref[v], stage_ref)
        for p in range(16):
            w_ref[v, p] = stage_ref[pl.ds(p, 8, stride=16), :]
    pack_faces(
        lambda v, p: w_ref[v, p],
        lax.axis_index("gx") % 2,
        lax.axis_index("gy") % 2,
        xa_ref,
        xb_ref,
        ya_ref,
        yb_ref,
    )


def selection(i, khalf):
    column = lax.broadcasted_iota(jnp.int32, (64, 128), 0)
    lane = lax.broadcasted_iota(jnp.int32, (64, 128), 1)
    hit = (column == 2 * (lane // 4) + khalf) & (lane % 4 == i)
    return hit.astype(jnp.float32)


def coefficient_kernel(
    flux_ref, speed_ref, source_ref, wall_ref, turbine_ref, thrust_ref, mix_ref, diag_ref, aux_ref, stage_ref
):
    lane, sub = lanes(), sublanes()
    dot = lambda x, y: jnp.dot(x, y, precision=EXACT, preferred_element_type=jnp.float32)
    speed_halves = []
    for khalf in range(2):
        total = jnp.zeros((108, 128), jnp.float32)
        speed = jnp.zeros((8, 128), jnp.float32)
        for i in range(4):
            select = selection(i, khalf)
            total = total + dot(flux_ref[pl.ds(i, 108, stride=4), :], select)
            speed = speed + dot(jnp.broadcast_to(speed_ref[i : i + 1, :], (8, 64)), select)
        for slot in range(4):
            mix_ref[pl.ds(slot * 2 + khalf, 108, stride=8), :] = total
        speed_halves.append(speed)
    speed3 = 3.0 * jnp.where(sub % 2 == 0, speed_halves[0], speed_halves[1])
    wall = jnp.zeros((8, 128), jnp.float32)
    for i in range(4):
        row = lax.broadcasted_iota(jnp.int32, (16, 128), 0)
        col = lax.broadcasted_iota(jnp.int32, (16, 128), 1)
        select = (col == row * 8 + i).astype(jnp.float32)
        flags = jnp.broadcast_to(wall_ref[i : i + 1, :].astype(jnp.float32), (8, 16))
        wall = wall + dot(flags, select)
    wall = jnp.where(sub == 0, wall, 0.0)
    kappa = jnp.zeros((8, 128), jnp.float32)
    for r in range(4):
        elem = turbine_ref[r : r + 1, :]
        columns = 64 * lax.axis_size("gy")
        row = (elem >> (columns.bit_length() - 1)) - lax.axis_index("gx") * 4
        col = (elem & (columns - 1)) - lax.axis_index("gy") * 64
        inside = (row >= 0) & (row < 4) & (col >= 0) & (col < 64)
        code = jnp.where(inside, (col >> 1) * 4 + row, -1)
        khalf = jnp.broadcast_to(jnp.where(inside, col & 1, -1), (8, 128))
        weight = jnp.where(khalf == sub % 2, jnp.broadcast_to(thrust_ref[r : r + 1, :], (8, 128)), 0.0)
        match = lax.broadcasted_iota(jnp.int32, (128, 128), 0) == jnp.broadcast_to(code, (128, 128))
        kappa = kappa + lax.dot_general(
            weight,
            match.astype(jnp.float32),
            (((1,), (1,)), ((), ())),
            precision=EXACT,
            preferred_element_type=jnp.float32,
        )
    zero = jnp.zeros((8, 128), jnp.float32)
    aux_ref[0] = speed3
    aux_ref[1] = 3.0 * wall
    for turn in range(1, 4):
        table = zero
        for slot in range(4):
            entry = DHAT[SLOTS[(slot - turn) % 4], SLOTS[slot]]
            table = jnp.where(sub // 2 == slot, jnp.float32(entry), table)
        aux_ref[1 + turn] = table
    aux_ref[5] = jnp.where(sub // 2 == 0, 3.0, jnp.where(sub // 2 == 2, -3.0, zero))
    ends_z = jnp.where(sub // 2 == 0, 1.0, jnp.where(sub // 2 == 2, 1.0, zero)) + wall
    for v in range(6):
        into_layout(source_ref[v], stage_ref)
        extra = kappa - SHIFT if v in (1, 2, 3) else zero - SHIFT
        bases = [extra + speed3 * (ends_z + float(n)) for n in range(3)]
        for p in range(16):
            faces = (p % 4 in (0, 3)) + (p // 4 in (0, 3))
            diag_ref[v, p] = stage_ref[pl.ds(p, 8, stride=16), :] + bases[faces]


def line_terms(values, below, above):
    d = [[float(np.float32(DHAT[q, p])) for p in range(4)] for q in range(4)]
    out = []
    for p in range(4):
        total = None
        for q in range(4):
            if q != p:
                term = d[q][p] * values[q]
                total = term if total is None else total + term
        out.append(total)
    out[0] = out[0] + 3.0 * below
    out[3] = out[3] - 3.0 * above
    return out


def apply_kernel(order, *refs):
    basis, refs = refs[:order], refs[order:]
    (xa_in, xb_in, ya_in, yb_in, mix_ref, diag_ref, aux_ref), refs = refs[:7], refs[7:]
    if order < 3:
        w_out, xa_out, xb_out, ya_out, yb_out, dots_ref, g_ref = refs
    else:
        dots1_ref, dots2_ref, sum_ref, g_ref, w_out = refs
    w_in = basis[-1]
    lane, sub = lanes(), sublanes()
    parity_x, parity_y = lax.axis_index("gx") % 2, lax.axis_index("gy") % 2
    speed3, wall3 = aux_ref[0], aux_ref[1]
    turns = [aux_ref[2], aux_ref[3], aux_ref[4]]
    ends = aux_ref[5]
    khigh = (lane // 4) % 2
    y_below = [jnp.where(parity_y == 0, yb_in[h], ya_in[h]) for h in range(2)]
    y_above = [jnp.where(parity_y == 0, ya_in[h], yb_in[h]) for h in range(2)]
    for v in range(6):
        w = [w_in[v, p] for p in range(16)]
        jump = [None] * 16

        def add_jump(p, value):
            jump[p] = value if jump[p] is None else jump[p] + value

        x_below = jnp.where(parity_x == 0, xb_in[v], xa_in[v])
        x_above = jnp.where(parity_x == 0, xa_in[v], xb_in[v])
        for b in range(4):
            below = jnp.where(lane % 4 == 0, roll(x_below, -b, 1), roll(w[b * 4 + 3], 1, 1))
            above = jnp.where(lane % 4 == 3, roll(x_above, 3 - b, 1), roll(w[b * 4], -1, 1))
            terms = line_terms([w[b * 4 + a] for a in range(4)], below, above)
            for a in range(4):
                g_ref[0, v, b * 4 + a] = terms[a]
            add_jump(b * 4, below)
            add_jump(b * 4 + 3, above)
        for a in range(4):
            slot = (v % 4) * 4 + a
            below = jnp.where(lane < 8, roll(y_below[v // 4], -8 * slot, 1), roll(w[12 + a], 8, 1))
            above = jnp.where(lane >= 120, roll(y_above[v // 4], 120 - 8 * slot, 1), roll(w[a], -8, 1))
            terms = line_terms([w[b * 4 + a] for b in range(4)], below, above)
            for b in range(4):
                g_ref[1, v, b * 4 + a] = terms[b]
            add_jump(a, below)
            add_jump(12 + a, above)
        for p in range(16):
            up3, up5 = roll(w[p], 3, 0), roll(w[p], 5, 0)
            near = jnp.where(
                (sub == 0) & (khigh == 1),
                roll(up3, 4, 1),
                jnp.where((sub == 5) & (khigh == 0), roll(up5, -4, 1), 0.0),
            )
            near = jnp.where(sub == 1, up5, jnp.where(sub == 4, up3, near))
            term = wall3 * w[p] + ends * near
            for turn in range(1, 4):
                term = term + turns[turn - 1] * roll(w[p], 2 * turn, 0)
            g_ref[2, v, p] = term
            add_jump(p, near)
            w_out[v, p] = diag_ref[v, p] * w[p] - speed3 * jump[p]

    def mix(p, sums):
        inputs = [g_ref[d, v, p] for d in range(3) for v in range(6)]
        new = [None] * (order + 1)
        for u in range(6):
            total = w_out[u, p]
            for n in range(18):
                total = total + mix_ref[n * 6 + u] * inputs[n]
            w_out[u, p] = total
            others = [ref[u, p] for ref in basis] + [total]
            for m in range(order + 1):
                product = others[m] * total
                new[m] = product if u == 0 else new[m] + product
        if order == 1:
            first = None
            for u in range(6):
                value = w_in[u, p]
                first = value * value if u == 0 else first + value * value
            new = [first] + new
        return tuple(s + n for s, n in zip(sums, new))

    count = order + 1 + (order == 1)
    sums = lax.fori_loop(0, 16, mix, (jnp.zeros((8, 128), jnp.float32),) * count)
    rows = [jnp.sum(s, axis=0, keepdims=True) for s in sums]
    rows = [row + roll(row, 64, 1) for row in rows]
    if order < 3:
        out = jnp.zeros((8, 128), jnp.float32)
        for m in range(count):
            out = jnp.where(sub == m, jnp.broadcast_to(rows[m], (8, 128)), out)
        dots_ref[...] = out
        pack_faces(lambda v, p: w_out[v, p], parity_x, parity_y, xa_out, xb_out, ya_out, yb_out)
    else:
        all_rows = [dots1_ref[m : m + 1, :] for m in range(3)]
        all_rows += [dots2_ref[m : m + 1, :] for m in range(3)] + rows
        out = jnp.zeros((8, 128), jnp.float32)
        for m, row in enumerate(all_rows):
            out = jnp.where(
                (sub == m % 8) & (lane // 64 == m // 8), jnp.broadcast_to(row, (8, 128)), out
            )
        for peer in range(sum_ref.shape[0]):
            sum_ref[peer] = out


def two_sum(a, b):
    total = a + b
    back = total - a
    return total, (a - (total - back)) + (b - back)


def halves(a):
    scaled = a * 4097.0
    high = scaled - (scaled - a)
    return high, a - high


class Pair:
    def __init__(self, high, low=None):
        self.high = high
        self.low = jnp.zeros_like(high) if low is None else low

    def __add__(self, other):
        total, error = two_sum(self.high, other.high)
        error = error + (self.low + other.low)
        high = total + error
        return Pair(high, error - (high - total))

    def __neg__(self):
        return Pair(-self.high, -self.low)

    def __sub__(self, other):
        return self + (-other)

    def __mul__(self, other):
        product = self.high * other.high
        ah, al = halves(self.high)
        bh, bl = halves(other.high)
        error = ((ah * bh - product) + ah * bl + al * bh) + al * bl
        error = error + (self.high * other.low + self.low * other.high)
        high = product + error
        return Pair(high, error - (high - product))

    def __truediv__(self, other):
        first = self.high / other.high
        rest = self - Pair(first) * other
        second = rest.high / other.high
        high = first + second
        return Pair(high, second - (high - first))

    def at_least_zero(self):
        keep = self.high > 0.0
        return Pair(jnp.where(keep, self.high, 0.0), jnp.where(keep, self.low, 0.0))


def least_squares(hessenberg, beta_norm, iters):
    cosines, sines, triangle = ([], [], [])
    target = [beta_norm] + [0.0 * beta_norm for index in range(iters)]
    for j in range(iters):
        column = list(hessenberg[j])
        for i in range(j):
            first_val, second_val = (column[i], column[i + 1])
            column[i] = cosines[i] * first_val + sines[i] * second_val
            column[i + 1] = -sines[i] * first_val + cosines[i] * second_val
        radius = jnp.sqrt(column[j] * column[j] + column[j + 1] * column[j + 1])
        cosines.append(column[j] / radius)
        sines.append(column[j + 1] / radius)
        column[j] = radius
        triangle.append(column[: j + 1])
        previous = target[j]
        target[j] = cosines[j] * previous
        target[j + 1] = -sines[j] * previous
    combination = [None] * iters
    for j in reversed(range(iters)):
        partial_sum = target[j]
        for k in range(j + 1, iters):
            partial_sum = partial_sum - triangle[k][j] * combination[k]
        combination[j] = partial_sum / triangle[j][j]
    return combination


def combination_of(gram):
    g00, g01, g11, g02, g12, g22, g03, g13, g23, g33 = gram
    one = jnp.ones_like(g00.high)
    eps = Pair(one * np.float32(EPS), one * np.float32(EPS - float(np.float32(EPS))))
    shift = Pair(one * SHIFT)
    n0 = g00 + eps
    s0 = (shift * eps - g01) / n0
    m01 = (g01 + shift * g00) * eps / n0
    m11 = (g11 + s0 * (g01 + m01)).at_least_zero()
    n1 = m11 + eps * n0
    w1p1 = g11 + s0 * g01
    w1u = g12 + s0 * g11
    up0 = g02 + s0 * g01
    up1 = w1u + s0 * up0
    uu = g22 + s0 * (g12 + w1u)
    k0 = shift * m01 + up0
    beta = -(k0 / n0)
    alpha = (shift * eps * n0 - up1) / n1
    m02 = up0 + alpha * m01 + beta * g00
    m12 = up1 + alpha * m11 + beta * m01
    m22 = (uu + alpha * (up1 + m12) + beta * (up0 + m02)).at_least_zero()
    n2 = m22 + eps * n1
    xp0 = g03 + s0 * g02
    xw1 = g13 + s0 * g12
    xp1 = xw1 + s0 * xp0
    xu = (g23 + s0 * g22) + s0 * xw1
    xx = g33 + s0 * (g23 + (g23 + s0 * g22))
    tp0 = xp0 + alpha * up0 + beta * g01
    tp1 = xp1 + alpha * up1 + beta * w1p1
    tu = xu + alpha * uu + beta * w1u
    tx = xx + alpha * xu + beta * xw1
    tw1 = xw1 + alpha * w1u + beta * g11
    tp2 = tu + alpha * tp1 + beta * tp0
    tt = tx + alpha * tu + beta * tw1
    k1 = shift * m12 + tp1
    k2 = shift * m02 + tp0
    beta2 = -(k1 / n1)
    gamma2 = -(k2 / n0)
    alpha2 = (shift * eps * n1 - tp2) / n2
    e0 = tp0 + alpha2 * m02 + beta2 * m01 + gamma2 * g00
    e1 = tp1 + alpha2 * m12 + beta2 * m11 + gamma2 * m01
    e2 = tp2 + alpha2 * m22 + beta2 * m12 + gamma2 * m02
    m33 = tt + alpha2 * (tp2 + e2) + beta2 * (tp1 + e1) + gamma2 * (tp0 + e0)
    n3 = m33.at_least_zero() + eps * n2
    r0, r1, r2, r3 = (jnp.sqrt(n.high) for n in (n0, n1, n2, n3))
    hessenberg = [
        [SHIFT - s0.high, r1 / r0],
        [k0.high / (r0 * r1), SHIFT - alpha.high, r2 / r1],
        [k2.high / (r0 * r2), k1.high / (r1 * r2), SHIFT - alpha2.high, r3 / r2],
    ]
    y = least_squares(hessenberg, r0, 3)
    z0, z1, z2 = y[0] / r0, y[1] / r1, y[2] / r2
    s, al, be = s0.high, alpha.high, beta.high
    return z0 + s * z1 + (al * s + be) * z2, z1 + (s + al) * z2, z2


def finish_kernel(parts_ref, w0_ref, w1_ref, w2_ref, out_ref, stage_ref):
    total = Pair(parts_ref[0])
    for peer in range(1, parts_ref.shape[0]):
        total = total + Pair(parts_ref[peer])
    for by in (32, 16, 8, 4, 2, 1):
        total = total + Pair(roll(total.high, by, 1), roll(total.low, by, 1))
    gram = []
    for m in range(10):
        row, col = m % 8, 63 + 64 * (m // 8)
        gram.append(
            Pair(
                *(
                    jnp.broadcast_to(part[row : row + 1, col : col + 1], (8, 128))
                    for part in (total.high, total.low)
                )
            )
        )
    c0, c1, c2 = combination_of(gram)
    for v in range(6):
        for p in range(16):
            value = c0 * w0_ref[v, p] + c1 * w1_ref[v, p] + c2 * w2_ref[v, p]
            stage_ref[pl.ds(p, 8, stride=16), :] = value
        blocks = [
            stage_ref[block_of(khalf, c) : block_of(khalf, c) + 16, :]
            for khalf in range(2)
            for c in range(4)
        ]
        out_ref[v] = jnp.concatenate(blocks, 0).T


def vmem(count):
    return [pl.BlockSpec(memory_space=pltpu.VMEM)] * count


def call(kernel, outs, args, scratch=()):
    return pl.pallas_call(
        kernel,
        out_shape=outs,
        in_specs=vmem(len(args)),
        out_specs=jax.tree.map(lambda _: pl.BlockSpec(memory_space=pltpu.VMEM), outs),
        scratch_shapes=list(scratch),
        compiler_params=PARAMS,
    )(*args)


def swap(value, axis, odd, periodic):
    count = lax.axis_size(axis)
    pairs = []
    for i in range(count):
        peer = i + 1 if (i % 2 == 1) == odd else i - 1
        if periodic:
            peer %= count
        if 0 <= peer < count:
            pairs.append((i, peer))
    return lax.ppermute(value, axis, pairs)


def exchange(packs):
    xa, xb, ya, yb = packs
    return [
        swap(xa, "gx", False, False),
        swap(xb, "gx", True, False),
        swap(ya, "gy", False, True),
        swap(yb, "gy", True, True),
    ]


def to_rows(field):
    return field.reshape(6, 4, 32, 128).transpose(0, 2, 1, 3).reshape(6, 128, 128)


def from_rows(field):
    return field.reshape(6, 32, 4, 128).transpose(0, 2, 1, 3).reshape(6, 4, 4096)


def on_device(right_side, flux_jac, wave_speed, source, wall_flag, turbine_elem, disc_coef):
    tile = pltpu.VMEM((128, 128), jnp.float32)
    g_scratch = pltpu.VMEM((3, 6, 16, 8, 128), jnp.float32)
    packs_type = [XPACK, XPACK, YPACK, YPACK]
    w0, *packs = call(start_kernel, [FIELD, *packs_type], [to_rows(right_side)], [tile])
    halo = exchange(packs)
    mix, diag, aux = call(
        coefficient_kernel,
        [
            jax.ShapeDtypeStruct((864, 128), jnp.float32),
            FIELD,
            jax.ShapeDtypeStruct((6, 8, 128), jnp.float32),
        ],
        [
            flux_jac.reshape(432, 64),
            wave_speed,
            to_rows(source),
            wall_flag,
            turbine_elem.reshape(4, 128),
            disc_coef.reshape(4, 128),
        ],
        [tile],
    )
    mix = mix.reshape(108, 8, 128)
    basis, dots = [w0], []
    for order in (1, 2):
        w, *packs, d = call(
            lambda *refs, order=order: apply_kernel(order, *refs),
            [FIELD, *packs_type, DOTS],
            [*basis, *halo, mix, diag, aux],
            [g_scratch],
        )
        basis.append(w)
        dots.append(d)
        halo = exchange(packs)

    peers_x, peers_y = lax.axis_size("gx"), lax.axis_size("gy")

    def last(*refs):
        *ins, d1, d2, sum_ref, g_ref, w_ref = refs
        apply_kernel(3, *ins, d1, d2, sum_ref, g_ref, w_ref)

    sums = call(
        last,
        jax.ShapeDtypeStruct((peers_y, 8, 128), jnp.float32),
        [*basis, *halo, mix, diag, aux, *dots],
        [g_scratch, pltpu.VMEM((6, 16, 8, 128), jnp.float32)],
    )
    sums = lax.all_to_all(sums, "gy", 0, 0)
    sums = jnp.broadcast_to(jnp.sum(sums, 0)[None], (peers_x, 8, 128))
    sums = lax.all_to_all(sums, "gx", 0, 0)
    out = call(
        finish_kernel, jax.ShapeDtypeStruct((6, 128, 128), jnp.float32), [sums, *basis], [tile]
    )
    return from_rows(out)


def solution(mesh):
    in_specs = (
        P(None, "gx", "gy"),
        P(None, None, None, "gx", "gy"),
        P("gx", "gy"),
        P(None, "gx", "gy"),
        P("gx", "gy"),
        P(),
        P(),
    )
    out_specs = P(None, "gx", "gy")
    return jax.shard_map(
        on_device, mesh=mesh, in_specs=in_specs, out_specs=out_specs, check_vma=False
    )
```
